32 devices in a mesh: rep: 2 (over x), pts: 16 (over z, y, core).
Axes of the slice: x: 2, y: 2, z: 4, core: 2. Of those that a mesh axis runs over, the one named last changes fastest.
Arguments:
- fine_points: bfloat16 [32768, 256], P(('rep', 'pts')), may hold values from -6 to 6
- parent: int32 [32768], P(('rep', 'pts')), may hold values from 0 to 8191, as said below
- patch_count: int32 [32], P(('rep', 'pts')), may hold values from 512 to 1024
- qkv_fine: bfloat16 [256, 768], replicated, may hold values from -0.375 to 0.375
- out_fine: bfloat16 [256, 256], replicated, may hold values from -0.375 to 0.375
- pool_weight: bfloat16 [256, 512], replicated, may hold values from -0.375 to 0.375
- qkv_coarse: bfloat16 [512, 1536], replicated, may hold values from -0.25 to 0.25
- out_coarse: bfloat16 [512, 512], replicated, may hold values from -0.25 to 0.25
- cotangent: bfloat16 [8192, 512], P(('rep', 'pts')), may hold values from -6 to 6
Outputs:
- coarse_out: bfloat16 [8192, 512], P(('rep', 'pts'))
- grad_out_fine: bfloat16 [256, 256], replicated
- grad_pool: bfloat16 [256, 512], replicated
- grad_qkv_coarse: bfloat16 [512, 1536], replicated
- grad_out_coarse: bfloat16 [512, 512], replicated
The draws below stay inside these ranges and needn't reach their ends.
Inputs may be any that keep to these rules, and one draw needn't show every extreme that they name: `parent`: along the points of block b, parents never fall and lie in pooled rows b * 256 to (b + 1) * 256 + 31; the last block of each replica (pts index 15) keeps its parents in its own 256 rows.
All inputs are finite; a program needn't handle non-finite values.
Results may differ from the reference program's by a relative error of at most 0.018.
Values may be sent and summed in bfloat16 or wider, within the bound.
No kernel may reach another device: no remote copies, remote signals or barrier semaphores. Data moves between devices by JAX's collectives and lax.ppermute only.
A program may use at most 128 MiB of HBM per device.

```python
import jax
import jax.numpy as jnp
from jax import lax

C1 = 256
C2 = 512
HD = 16
PATCH = 1024
P_DEV = 1024
Q_DEV = 256
SPILL = 32
NP = 32768
NQ = 8192
NPATCH = 32
N_REP = 2
N_PTS = 16


def draw_parent(key, part):
    devices = N_REP * N_PTS
    reach = jnp.where(jnp.arange(devices) % N_PTS == N_PTS - 1, Q_DEV, Q_DEV + SPILL)
    raw_bits = jax.random.randint(jax.random.fold_in(key, 17), (devices, P_DEV), 0, 1 << 20)
    picker = jax.random.randint(jax.random.fold_in(key, 29), (devices, P_DEV), 0, 10)
    spilling = (picker < 3) & (reach > Q_DEV)[:, None]
    spill_pick = Q_DEV + raw_bits % SPILL
    spread_pick = raw_bits % reach[:, None]
    offsets = jnp.sort(jnp.where(spilling, spill_pick, spread_pick), axis=1)
    return (offsets + jnp.arange(devices)[:, None] * Q_DEV).reshape(-1).astype(jnp.int32)


def place_ends(values, rng, low, high):
    extent = values.shape
    index_at = [jax.random.randint(jax.random.fold_in(rng, axis), (), 0, extent[axis]) for axis in range(len(extent))]
    values = values.at[tuple(index_at)].set(low)
    longest = extent.index(max(extent))
    index_at[longest] = (index_at[longest] + 1) % extent[longest]
    return values.at[tuple(index_at)].set(high)


def block_scale(rng, shape, pieces, least, largest):
    def one(dim, parts):
        draws = jax.random.uniform(jax.random.fold_in(jax.random.fold_in(rng, 6), dim), (parts,), jnp.float32, least / len(pieces), largest / len(pieces))
        return jnp.repeat(jnp.exp(draws), shape[dim] // parts).reshape((-1,) + (1,) * (len(shape) - dim - 1))

    level = one(*pieces[0])
    for cut in pieces[1:]:
        level = level * one(*cut)
    return level


def normal_values(own_key, extent, spread, most, split=(), held_as=jnp.bfloat16):
    result = jax.random.normal(own_key, extent, jnp.float32) * spread
    if len(split) > 0:
        result = block_scale(own_key, extent, split, -0.22, 0.18) * result
    return jnp.clip(result, min=-most, max=most).astype(held_as)


def setup_inputs(seed: int = 0) -> dict:
    keys = jax.random.split(jax.random.key(seed), 10)
    return {
        "fine_points": normal_values(keys[0], (NP, C1), 1.0, 6.0, ((0, 32),)),
        "parent": draw_parent(jax.random.fold_in(keys[9], 71), 0),
        "patch_count": place_ends(jax.random.randint(keys[2], (NPATCH,), PATCH // 2, PATCH + 1), jax.random.fold_in(keys[2], 1), PATCH // 2, PATCH).astype(jnp.int32),
        "qkv_fine": normal_values(keys[3], (C1, 3 * C1), C1 ** -0.5, 0.375),
        "out_fine": normal_values(keys[4], (C1, C1), C1 ** -0.5, 0.375),
        "pool_weight": normal_values(keys[5], (C1, C2), C1 ** -0.5, 0.375),
        "qkv_coarse": normal_values(keys[6], (C2, 3 * C2), C2 ** -0.5, 0.25),
        "out_coarse": normal_values(keys[7], (C2, C2), C2 ** -0.5, 0.25),
        "cotangent": normal_values(keys[8], (NQ, C2), 1.0, 6.0, ((0, 32),)),
    }


epsilon = 1e-06
logit_scale = 0.25

def normalize(values):
    return values * lax.rsqrt(lax.optimization_barrier(jnp.mean(values * values, axis=-1, keepdims=True)) + epsilon)

def attend(queries, key_rows, value_rows, head_count, key_mask):
    query_rows = queries.shape[0]
    key_total = key_rows.shape[0]
    channels = queries.shape[1]
    head_size = channels // head_count
    group = min(4, head_count)
    groups = head_count // group
    head_query = queries.reshape(query_rows, groups, group, head_size).transpose(1, 0, 2, 3)
    head_key = key_rows.reshape(key_total, groups, group, head_size).transpose(1, 0, 2, 3)
    head_value = value_rows.reshape(key_total, groups, group, head_size).transpose(1, 0, 2, 3)

    @jax.checkpoint
    def one_group(element):
        grouped_query_rows, grouped_key_rows, grouped_value_rows = element
        logit_table = jnp.einsum('ygq,pgq->gyp', grouped_query_rows, grouped_key_rows, preferred_element_type=jnp.float32) * logit_scale
        if key_mask is not None:
            logit_table = jnp.where(key_mask[None, None, :], logit_table, -1e+30)
        logit_table = logit_table - lax.stop_gradient(lax.optimization_barrier(jnp.max(logit_table, axis=-1, keepdims=True)))
        exponent = jnp.exp(logit_table)
        attention_weight = (exponent / lax.optimization_barrier(jnp.sum(exponent, axis=-1, keepdims=True))).astype(jnp.bfloat16)
        grouped_mixture = jnp.einsum('yex,xyb->eyb', attention_weight, grouped_value_rows, preferred_element_type=jnp.float32)
        return grouped_mixture.astype(jnp.bfloat16)
    mixed_rows = lax.map(one_group, (head_query, head_key, head_value))
    return mixed_rows.transpose(1, 0, 2, 3).reshape(query_rows, channels)

def fine_attention(tokens, qkv_weight, patch_count):
    channels = tokens.shape[1]
    normed = normalize(tokens.astype(jnp.float32)).astype(jnp.bfloat16)
    packed = jnp.dot(normed, qkv_weight, preferred_element_type=jnp.float32).astype(jnp.bfloat16)
    slot_count = tokens.shape[0] // PATCH
    blocks = packed.reshape(slot_count, PATCH, 3 * channels)

    def one_patch(element):
        patch_rows, length = element
        key_mask = jnp.arange(PATCH) < length
        return attend(patch_rows[:, :channels], patch_rows[:, channels:2 * channels], patch_rows[:, 2 * channels:], channels // HD, key_mask)
    return lax.map(one_patch, (blocks, patch_count)).reshape(tokens.shape[0], channels)

def parent_table(offset):
    return (offset[:, None] == jnp.arange(Q_DEV + SPILL, dtype=jnp.int32)[None, :]).astype(jnp.float32)

def pool_counts(live_mask, offset):
    return jnp.dot(live_mask[None, :], parent_table(offset), precision=lax.Precision.HIGHEST)[0]

def pool_forward(out_weight, pooling, tokens, mixed_rows, live_mask, offset):
    fine_out = (tokens.astype(jnp.float32) + jnp.dot(mixed_rows, out_weight.astype(jnp.bfloat16), preferred_element_type=jnp.float32)).astype(jnp.bfloat16)
    projected = jnp.dot(fine_out, pooling.astype(jnp.bfloat16), preferred_element_type=jnp.float32) * live_mask[:, None]
    summed = jnp.dot(parent_table(offset).T, projected, precision=lax.Precision.HIGHEST)
    return (summed[:Q_DEV], summed[Q_DEV:])

def coarse_forward(own_sum, arrived, qkv_weight, divisor):
    summed = own_sum + jnp.pad(arrived, ((0, Q_DEV - SPILL), (0, 0)))
    coarse_in = jax.nn.gelu(summed / divisor[:, None]).astype(jnp.bfloat16)
    normed = normalize(coarse_in.astype(jnp.float32)).astype(jnp.bfloat16)
    packed = jnp.dot(normed, qkv_weight.astype(jnp.bfloat16), preferred_element_type=jnp.float32).astype(jnp.bfloat16)
    channels = coarse_in.shape[1]
    return (coarse_in, packed[:, :channels], packed[:, channels:2 * channels], packed[:, 2 * channels:])

def coarse_attention(coarse_in, queries, key_rows, value_rows, far_keys, far_values, out_weight):
    all_keys = jnp.concatenate([key_rows, far_keys], 0).astype(jnp.bfloat16)
    all_values = jnp.concatenate([value_rows, far_values], 0).astype(jnp.bfloat16)
    mixed_rows = attend(queries, all_keys, all_values, queries.shape[1] // HD, None)
    return (coarse_in.astype(jnp.float32) + jnp.dot(mixed_rows, out_weight.astype(jnp.bfloat16), preferred_element_type=jnp.float32)).astype(jnp.bfloat16)

def reference(fine_points, parent, patch_count, qkv_fine, out_fine, pool_weight, qkv_coarse, out_coarse, cotangent):
    devices = N_REP * N_PTS
    slot_count = P_DEV // PATCH
    channels = fine_points.shape[1]
    coarse_width = qkv_coarse.shape[0]
    tokens_all = fine_points.reshape(devices, P_DEV, channels)
    offsets = (parent.reshape(devices, P_DEV) - (jnp.arange(devices, dtype=jnp.int32) * Q_DEV)[:, None]).astype(jnp.int32)
    counts_all = patch_count.reshape(devices, slot_count)
    out_fine_wide = out_fine.astype(jnp.float32)
    pool_wide = pool_weight.astype(jnp.float32)
    qkv_wide = qkv_coarse.astype(jnp.float32)
    out_coarse_wide = out_coarse.astype(jnp.float32)

    def first_pass(element):
        tokens, offset, length = element
        mixed_rows = fine_attention(tokens, qkv_fine, length)
        live_mask = (jnp.arange(PATCH)[None, :] < length[:, None]).reshape(P_DEV).astype(jnp.float32)
        live_total = pool_counts(live_mask, offset)
        own_sum, spill_sum = pool_forward(out_fine_wide, pool_wide, tokens, mixed_rows, live_mask, offset)
        return (mixed_rows, live_mask, own_sum, spill_sum, live_total)
    mixed_all, live_all, own_all, spill_all, live_totals = lax.map(first_pass, (tokens_all, offsets, counts_all))

    def shift_down(stacked):
        grouped = stacked.reshape((N_REP, N_PTS) + stacked.shape[1:])
        moved = jnp.concatenate([jnp.zeros_like(grouped[:, :1]), grouped[:, :-1]], 1)
        return moved.reshape(stacked.shape)

    def shift_up(stacked):
        grouped = stacked.reshape((N_REP, N_PTS) + stacked.shape[1:])
        moved = jnp.concatenate([grouped[:, 1:], jnp.zeros_like(grouped[:, :1])], 1)
        return moved.reshape(stacked.shape)

    def swap_pairs(stacked):
        grouped = stacked.reshape((devices // 2, 2) + stacked.shape[1:])
        return grouped[:, ::-1].reshape(stacked.shape)
    arrived_all = shift_down(spill_all)
    arrived_counts = shift_down(live_totals[:, Q_DEV:])
    divisors = jnp.maximum(live_totals[:, :Q_DEV] + jnp.pad(arrived_counts, ((0, 0), (0, Q_DEV - SPILL))), 1.0)

    def second_pass(element):
        own_sum, arrived, divisor = element
        return coarse_forward(own_sum, arrived, qkv_wide, divisor)
    coarse_in_all, query_all, key_all, value_all = lax.map(second_pass, (own_all, arrived_all, divisors))
    far_key_all = swap_pairs(key_all)
    far_value_all = swap_pairs(value_all)

    def third_pass(element):
        coarse_in, queries, key_rows, value_rows, far_keys, far_values, grad_out = element
        coarse_rows, backward = jax.vjp(coarse_attention, coarse_in, queries, key_rows.astype(jnp.float32), value_rows.astype(jnp.float32), far_keys.astype(jnp.float32), far_values.astype(jnp.float32), out_coarse_wide)
        return (coarse_rows,) + tuple(backward(grad_out))
    grad_rows = cotangent.reshape(devices, Q_DEV, coarse_width)
    results = lax.map(third_pass, (coarse_in_all, query_all, key_all, value_all, far_key_all, far_value_all, grad_rows))
    coarse_all, grad_in, grad_query, grad_key, grad_value, grad_far_key, grad_far_value, grad_out_coarse = results
    back_key = swap_pairs(grad_far_key.astype(jnp.bfloat16))
    back_value = swap_pairs(grad_far_value.astype(jnp.bfloat16))
    total_key = (grad_key + back_key.astype(jnp.float32)).astype(jnp.bfloat16)
    total_value = (grad_value + back_value.astype(jnp.float32)).astype(jnp.bfloat16)

    def fourth_pass(element):
        own_sum, arrived, divisor, grad_coarse_in, grad_queries, grad_keys, grad_values = element

        def local_part(own_part, arrived_part, qkv_part):
            return coarse_forward(own_part, arrived_part, qkv_part, divisor)
        unused, backward = jax.vjp(local_part, own_sum, arrived, qkv_wide)
        return backward((grad_coarse_in, grad_queries, grad_keys, grad_values))
    grad_own, grad_arrived, grad_qkv_coarse = lax.map(fourth_pass, (own_all, arrived_all, divisors, grad_in, grad_query, total_key, total_value))
    grad_spill = shift_up(grad_arrived)

    def fifth_pass(element):
        tokens, mixed_rows, live_mask, offset, grad_own_rows, grad_spill_rows = element

        def local_part(out_weight, pooling):
            return pool_forward(out_weight, pooling, tokens, mixed_rows, live_mask, offset)
        unused, backward = jax.vjp(local_part, out_fine_wide, pool_wide)
        return backward((grad_own_rows, grad_spill_rows))
    grad_out_fine, grad_pool = lax.map(fifth_pass, (tokens_all, mixed_all, live_all, offsets, grad_own, grad_spill))

    def reduce_all(stacked):
        grouped = stacked.astype(jnp.float32).reshape((N_REP, N_PTS) + stacked.shape[1:])
        group_sum = lax.optimization_barrier(lax.optimization_barrier(jnp.sum(grouped, 1)).astype(jnp.bfloat16)).astype(jnp.float32)
        return lax.optimization_barrier(jnp.sum(group_sum, 0)).astype(jnp.bfloat16)
    return (coarse_all.reshape(devices * Q_DEV, coarse_width), reduce_all(grad_out_fine), reduce_all(grad_pool), reduce_all(grad_qkv_coarse), reduce_all(grad_out_coarse))
```

```python
import functools

import jax
import jax.numpy as jnp
from jax import lax
from jax.experimental import pallas as pl
from jax.experimental.pallas import tpu as pltpu
from jax.sharding import PartitionSpec as P

HD = 16
SPILL = 32
EPS = 1e-06
LOG2E = 1.4426950408889634
LN2 = 0.6931471805599453
SCALE = 0.25
SAFE = 60.0
bf16 = jnp.bfloat16
f32 = jnp.float32
NT = (((1,), (1,)), ((), ()))


def mm(a, b):
    return jnp.dot(a, b, preferred_element_type=f32)


def mm_nt(a, b):
    return lax.dot_general(a, b, NT, preferred_element_type=f32)


def head_lane(width):
    return lax.broadcasted_iota(jnp.int32, (1, width), 1) // HD


def spread(per_head, rows):
    heads, cols = per_head.shape
    wide = jnp.broadcast_to(per_head[:, None, :], (heads, HD, cols))
    return wide.reshape(rows, cols)


def logit_bound(q_t, keys):
    channels, rows = q_t.shape
    q_f = q_t.astype(f32)
    q_sq = jnp.max(jnp.sum((q_f * q_f).reshape(channels // HD, HD, rows), axis=1))
    k_f = keys.astype(f32)
    member = (
        lax.broadcasted_iota(jnp.int32, (channels, 128), 0) // HD
        == lax.broadcasted_iota(jnp.int32, (channels, 128), 1)
    ).astype(bf16)
    k_sq = jnp.max(mm((k_f * k_f).astype(bf16), member))
    return q_sq * k_sq


def stage_values(vx_ref, v_t, live):
    channels, rows = v_t.shape
    first = lax.broadcasted_iota(jnp.int32, (HD, rows), 0) == 0
    ones = jnp.where(first, live, 0.0).astype(bf16)
    for h in range(channels // HD):
        vx_ref[h, 0:HD, :] = (v_t[h * HD : (h + 1) * HD, :] * live).astype(bf16)
        vx_ref[h, HD : 2 * HD, :] = ones


def fine_kernel(count_ref, x_ref, offset_ref, w_ref, wout_ref, out_ref, k_ref, q_ref, vx_ref, o_ref):
    points, channels = x_ref.shape
    heads = channels // HD
    rows = out_ref.shape[0]
    count = count_ref[0]
    x = x_ref[...].astype(f32)
    normed = (x * lax.rsqrt(jnp.mean(x * x, axis=-1, keepdims=True) + EPS)).astype(bf16)
    packed_q = mm(normed, w_ref[:, 0:channels]) * (SCALE * LOG2E)
    q_ref[...] = packed_q.T.astype(bf16)
    keys = mm(normed, w_ref[:, channels : 2 * channels]).astype(bf16)
    k_ref[...] = keys
    lane_point = lax.broadcasted_iota(jnp.int32, (1, points), 1)
    live = (lane_point < count).astype(f32)
    v_t = mm(normed, w_ref[:, 2 * channels :]).astype(bf16).astype(f32).T
    stage_values(vx_ref, v_t, live)
    safe = logit_bound(q_ref[...], keys) < SAFE * SAFE
    lane = head_lane(channels)

    def one_head(h, carry, shifted):
        k_h = jnp.where(lane == h, k_ref[...], jnp.zeros((), bf16))
        logits = mm(k_h, q_ref[...])
        if shifted:
            row = lax.broadcasted_iota(jnp.int32, (points, 1), 0)
            logits = jnp.where(row < count, logits, -1e30)
            logits = logits - jnp.max(logits, axis=0, keepdims=True)
        weights = jnp.exp2(logits).astype(bf16)
        o_ref[h] = mm(vx_ref[h], weights)
        return carry

    @pl.when(safe)
    def _():
        lax.fori_loop(0, heads, functools.partial(one_head, shifted=False), 0)

    @pl.when(jnp.logical_not(safe))
    def _():
        lax.fori_loop(0, heads, functools.partial(one_head, shifted=True), 0)

    o = o_ref[...]
    mixed = o[:, 0:HD, :] / o[:, HD : HD + 1, :]
    mixed = mixed.reshape(channels, points).T.astype(bf16)
    fine_out = (x + mm(mixed, wout_ref[...])).astype(bf16)
    pooled_row = lax.broadcasted_iota(jnp.int32, (rows, points), 0)
    table = ((pooled_row == offset_ref[...]) & (lane_point < count)).astype(f32).astype(bf16)
    out_ref[:, 0:channels] = mm(table, fine_out).astype(bf16)
    out_ref[:, channels : 2 * channels] = mm(table, mixed).astype(bf16)
    counted = mm(table, jnp.ones((points, 128), bf16))
    high = counted.astype(bf16).astype(f32)
    half = lax.broadcasted_iota(jnp.int32, (1, 128), 1) < 64
    out_ref[:, 2 * channels :] = jnp.where(half, high, counted - high).astype(bf16)


def fine_stage(x, offset, count, w_qkv, w_out, rows):
    points, channels = x.shape
    heads = channels // HD
    vmem = pl.BlockSpec(memory_space=pltpu.VMEM)
    return pl.pallas_call(
        fine_kernel,
        out_shape=jax.ShapeDtypeStruct((rows, 2 * channels + 128), bf16),
        in_specs=[pl.BlockSpec(memory_space=pltpu.SMEM), vmem, vmem, vmem, vmem],
        out_specs=vmem,
        scratch_shapes=[
            pltpu.VMEM((points, channels), bf16),
            pltpu.VMEM((channels, points), bf16),
            pltpu.VMEM((heads, 2 * HD, points), bf16),
            pltpu.VMEM((heads, 2 * HD, points), f32),
        ],
        compiler_params=pltpu.CompilerParams(vmem_limit_bytes=48 * 2**20),
        cost_estimate=pl.CostEstimate(
            flops=2 * points * points * channels * 2 * heads,
            bytes_accessed=4 * points * channels,
            transcendentals=heads * points * points,
        ),
        name="fine_stage",
    )(count, x, offset, w_qkv, w_out)


def gelu_parts(u):
    inner_scale = 0.7978845608028654
    cubic = 0.044715
    t = jnp.tanh(inner_scale * (u + cubic * u * u * u))
    value = 0.5 * u * (1.0 + t)
    slope = 0.5 * (1.0 + t) + 0.5 * u * (1.0 - t * t) * inner_scale * (1.0 + 3.0 * cubic * u * u)
    return value, slope


def coarse_kernel(
    core_ref, own_ref, far_ref, prev_ref, pool_ref, wq_ref, wk_ref, wv_ref, wout_ref,
    cot_own_ref, cot_far_ref,
    mixed_ref, center_ref, big_ref, small_ref,
    q_ref, qt_ref, k_ref, kt_ref, v_ref, vx_ref, p_ref, o_ref, do_ref, dot_ref, delta_ref,
    dqt_ref, dk_ref, dv_ref,
):
    own = cot_own_ref.shape[0]
    width = cot_own_ref.shape[1]
    channels = wq_ref.shape[1]
    c1 = pool_ref.shape[0]
    heads = channels // HD
    rows = 2 * own
    first_core = core_ref[0] == 0

    own_block = own_ref[...].astype(f32)
    far_block = far_ref[...].astype(f32)
    prev = prev_ref[...].astype(f32)
    own_spill = jnp.where(first_core, prev, far_block[own:, :])
    far_spill = jnp.where(first_core, own_block[own:, :], prev)
    table = jnp.concatenate(
        [
            own_block[0:SPILL] + own_spill,
            own_block[SPILL:own],
            far_block[0:SPILL] + far_spill,
            far_block[SPILL:own],
        ],
        axis=0,
    )
    counted = table[:, 2 * c1 : 2 * c1 + 1] + table[:, 2 * c1 + 64 : 2 * c1 + 65]
    share = 1.0 / jnp.maximum(counted, 1.0)
    pooled_x = table[:, 0:c1].astype(bf16)
    pooled_mix = table[:, c1 : 2 * c1].astype(bf16)
    value, slope = gelu_parts(mm(pooled_x, pool_ref[...]) * share)
    center = value.astype(bf16)
    center_ref[...] = center[0:own]
    center = center.astype(f32)
    root = lax.rsqrt(jnp.mean(center * center, axis=-1, keepdims=True) + EPS)
    normed = (center * root).astype(bf16)
    q2 = (mm(normed, wq_ref[...]) * (SCALE * LOG2E)).astype(bf16)
    q_ref[...] = q2
    qt_ref[...] = q2.astype(f32).T.astype(bf16)
    keys = mm(normed, wk_ref[...]).astype(bf16)
    k_ref[...] = keys
    kt_ref[...] = keys.astype(f32).T.astype(bf16)
    values = mm(normed, wv_ref[...]).astype(bf16)
    v_ref[...] = values
    stage_values(vx_ref, values.astype(f32).T, jnp.ones((1, rows), f32))
    safe = logit_bound(qt_ref[...], keys) < SAFE * SAFE
    lane = head_lane(channels)
    zero = jnp.zeros((), bf16)

    def forward_head(h, carry, shifted):
        k_h = jnp.where(lane == h, k_ref[...], zero)
        logits = mm(k_h, qt_ref[...])
        if shifted:
            logits = logits - jnp.max(logits, axis=0, keepdims=True)
        weights = jnp.exp2(logits).astype(bf16)
        p_ref[h] = weights
        o_ref[h] = mm(vx_ref[h], weights)
        return carry

    @pl.when(safe)
    def _():
        lax.fori_loop(0, heads, functools.partial(forward_head, shifted=False), 0)

    @pl.when(jnp.logical_not(safe))
    def _():
        lax.fori_loop(0, heads, functools.partial(forward_head, shifted=True), 0)

    o = o_ref[...]
    inverse = 1.0 / o[:, HD, :]
    mixed_t = o[:, 0:HD, :].reshape(channels, rows) * spread(inverse, channels)
    mixed_bf = mixed_t.astype(bf16)
    mixed_ref[...] = mixed_t.T.astype(bf16)
    cot = jnp.concatenate([cot_own_ref[...], cot_far_ref[...]], axis=0)
    do_t = mm_nt(wout_ref[...], cot)
    delta = jnp.sum((do_t * mixed_bf.astype(f32)).reshape(heads, HD, rows), axis=1)
    delta_ref[...] = (delta * inverse).reshape(heads, 1, rows)
    do_t = do_t * spread(inverse, channels)
    dot_ref[...] = do_t.astype(bf16)
    do_ref[...] = do_t.T.astype(bf16)
    dk_ref[...] = jnp.zeros_like(dk_ref)
    dv_ref[...] = jnp.zeros_like(dv_ref)

    def backward_head(h, carry):
        mask = lane == h
        v_h = jnp.where(mask, v_ref[...], zero)
        slopes = mm(v_h, dot_ref[...])
        weights = p_ref[h]
        ds = (weights.astype(f32) * (slopes - delta_ref[h])).astype(bf16)
        start = pl.multiple_of(h * HD, HD)
        dqt_ref[pl.ds(start, HD), :] = mm(kt_ref[pl.ds(start, HD), :], ds)
        dk_ref[...] += mm(ds, jnp.where(mask, q_ref[...], zero))
        dv_ref[...] += mm(weights, jnp.where(mask, do_ref[...], zero))
        return carry

    lax.fori_loop(0, heads, backward_head, 0)

    dq = (dqt_ref[...].T * SCALE).astype(bf16)
    dk = (dk_ref[...] * LN2).astype(bf16)
    dv = dv_ref[...].astype(bf16)
    normed_t = (center * root).T.astype(bf16)
    big_ref[0:width, :] = mm(normed_t, dq).astype(bf16)
    big_ref[width : 2 * width, :] = mm(normed_t, dk).astype(bf16)
    big_ref[2 * width : 3 * width, :] = mm(normed_t, dv).astype(bf16)
    grad_out = mm(mixed_bf, cot).astype(bf16)
    for i in range(width // channels):
        base = 3 * width + i * channels
        big_ref[base : base + channels, :] = grad_out[:, i * channels : (i + 1) * channels]

    dn = mm_nt(dq, wq_ref[...]) + mm_nt(dk, wk_ref[...]) + mm_nt(dv, wv_ref[...])
    dc = root * dn - center * (root * root * root) * jnp.mean(dn * center, axis=-1, keepdims=True)
    own_cot = cot_own_ref[...].astype(f32)
    dc = jnp.concatenate([dc[0:own] + own_cot, dc[own:]], axis=0)
    dpool = (dc * slope * share).astype(bf16)
    pooled_t = table[:, 0:c1].T.astype(bf16)
    mix_t = table[:, c1 : 2 * c1].T.astype(bf16)
    grad_pool = mm(pooled_t, dpool).astype(bf16)
    for i in range(width // c1):
        small_ref[i * c1 : (i + 1) * c1, :] = grad_pool[:, i * c1 : (i + 1) * c1]
    back = mm_nt(dpool, pool_ref[...]).astype(bf16)
    small_ref[width:, :] = mm(mix_t, back).astype(bf16)


def coarse_stage(core, own, far, prev, pool, w_qkv, w_out, cot_own, cot_far):
    q_rows, width = cot_own.shape
    rows = 2 * q_rows
    channels = width // 2
    c1 = pool.shape[0]
    heads = channels // HD

    def whole(shape):
        return pl.BlockSpec(shape, lambda i, core: (0, 0))

    def third(n):
        return pl.BlockSpec((width, channels), lambda i, core: (0, 2 * n + core[0]))

    out_shapes = (
        (rows, channels),
        (q_rows, width),
        (3 * width + width, channels),
        (width + c1, c1),
    )
    return pl.pallas_call(
        coarse_kernel,
        out_shape=tuple(jax.ShapeDtypeStruct(s, bf16) for s in out_shapes),
        grid_spec=pltpu.PrefetchScalarGridSpec(
            num_scalar_prefetch=1,
            grid=(1,),
            in_specs=[
                whole(own.shape), whole(far.shape), whole(prev.shape), whole(pool.shape),
                third(0), third(1), third(2),
                pl.BlockSpec((channels, width), lambda i, core: (core[0], 0)),
                whole(cot_own.shape), whole(cot_far.shape),
            ],
            out_specs=[whole(s) for s in out_shapes],
            scratch_shapes=[
                pltpu.VMEM((rows, channels), bf16),
                pltpu.VMEM((channels, rows), bf16),
                pltpu.VMEM((rows, channels), bf16),
                pltpu.VMEM((channels, rows), bf16),
                pltpu.VMEM((rows, channels), bf16),
                pltpu.VMEM((heads, 2 * HD, rows), bf16),
                pltpu.VMEM((heads, rows, rows), bf16),
                pltpu.VMEM((heads, 2 * HD, rows), f32),
                pltpu.VMEM((rows, channels), bf16),
                pltpu.VMEM((channels, rows), bf16),
                pltpu.VMEM((heads, 1, rows), f32),
                pltpu.VMEM((channels, rows), f32),
                pltpu.VMEM((rows, channels), f32),
                pltpu.VMEM((rows, channels), f32),
            ],
        ),
        compiler_params=pltpu.CompilerParams(vmem_limit_bytes=56 * 2**20),
        cost_estimate=pl.CostEstimate(
            flops=2 * rows * rows * channels * 5 * heads,
            bytes_accessed=4 * rows * width,
            transcendentals=heads * rows * rows,
        ),
        name="coarse_stage",
    )(core, own, far, prev, pool, w_qkv, w_qkv, w_qkv, w_out, cot_own, cot_far)


def route(value, hop):
    n_rep, n_pts = lax.axis_size("rep"), lax.axis_size("pts")
    pairs = [(i, i ^ hop(i)) for i in range(n_rep * n_pts)]
    return lax.ppermute(value, ("rep", "pts"), pairs)


def partner(value):
    return route(value, lambda i: 1)


def pieces(total, index, count):
    size = total.shape[0] // count
    return lax.dynamic_slice_in_dim(total, index * size, size, 0)


def sum_over_chips(value, flat):
    n_rep, n_pts = lax.axis_size("rep"), lax.axis_size("pts")
    rep_bits = [n_pts << b for b in range(n_rep.bit_length() - 1)]
    pts_bits = [1 << b for b in range(1, n_pts.bit_length() - 1)]
    orders = (rep_bits[:1] + pts_bits[:1], pts_bits[:1] + rep_bits[:1])
    rest = rep_bits[1:] + pts_bits[1:]
    steps = [(orders[0][s], orders[1][s]) for s in range(2)] + [(m, m) for m in rest]
    core = flat & 1
    kept = []
    for masks in steps:
        mask = jnp.where(core == 0, masks[0], masks[1])
        bit = (flat & mask != 0).astype(jnp.int32)
        arrived = route(pieces(value, 1 - bit, 2), lambda i: masks[i & 1])
        value = (pieces(value, bit, 2).astype(f32) + arrived.astype(f32)).astype(bf16)
        kept.append((masks, bit))
    for masks, bit in reversed(kept):
        arrived = route(value, lambda i: masks[i & 1])
        low = jnp.where(bit == 0, value, arrived)
        high = jnp.where(bit == 0, arrived, value)
        value = jnp.concatenate([low, high], axis=0)
    return value


def local(
    fine_points, parent, patch_count, qkv_fine, out_fine, pool_weight, qkv_coarse, out_coarse,
    cotangent,
):
    n_pts = lax.axis_size("pts")
    flat = lax.axis_index("rep") * n_pts + lax.axis_index("pts")
    core = flat & 1
    core_ref = core.reshape(1)
    q_dev, width = cotangent.shape
    channels = width // 2
    cot_far = partner(cotangent)
    offset = (parent - flat * q_dev)[None, :]
    own = fine_stage(fine_points, offset, patch_count, qkv_fine, out_fine, q_dev + SPILL)
    far = partner(own)
    last = jnp.where(core == 1, own[q_dev:], far[q_dev:])
    prev = lax.ppermute(last, "pts", [(i, i + 2) for i in range(n_pts - 2)])
    mixed, center, big, small = coarse_stage(
        core_ref, own, far, prev, pool_weight, qkv_coarse, out_coarse, cotangent, cot_far
    )
    mixed_far = partner(mixed[q_dev:])
    w_own = lax.dynamic_slice_in_dim(out_coarse, core * channels, channels, 0)
    w_far = lax.dynamic_slice_in_dim(out_coarse, (1 - core) * channels, channels, 0)
    coarse_rows = (center.astype(f32) + mm(mixed[:q_dev], w_own) + mm(mixed_far, w_far)).astype(bf16)

    small_sum = (
        pieces(small, core, 2).astype(f32) + partner(pieces(small, 1 - core, 2)).astype(f32)
    ).astype(bf16)
    mine = sum_over_chips(jnp.concatenate([big, small_sum], axis=0), flat)
    other = partner(mine)
    low = jnp.where(core == 0, mine, other)
    high = jnp.where(core == 0, other, mine)
    parts = []
    for n in range(3):
        parts += [low[n * width : (n + 1) * width], high[n * width : (n + 1) * width]]
    grad_qkv = jnp.concatenate(parts, axis=1)
    base = 3 * width

    def out_half(half):
        return jnp.concatenate(
            [half[base + i * channels : base + (i + 1) * channels] for i in range(2)], axis=1
        )

    grad_out = jnp.concatenate([out_half(low), out_half(high)], axis=0)
    tail = jnp.concatenate([low[base + width :], high[base + width :]], axis=0)
    c1 = pool_weight.shape[0]
    grad_pool = jnp.concatenate([tail[i * c1 : (i + 1) * c1] for i in range(width // c1)], axis=1)
    grad_fine = tail[width:]
    return coarse_rows, grad_fine, grad_pool, grad_qkv, grad_out


def solution(mesh):
    rows = P(("rep", "pts"), None)
    flat = P(("rep", "pts"))
    return jax.shard_map(
        local,
        mesh=mesh,
        in_specs=(rows, flat, flat, P(), P(), P(), P(), P(), rows),
        out_specs=(rows, P(), P(), P(), P()),
        check_vma=False,
    )
```
